32 devices in a mesh: dp: 4 (over y, x), ep: 8 (over z, core).
Axes of the slice: x: 2, y: 2, z: 4, core: 2. Of those that a mesh axis runs over, the one named last changes fastest.
Arguments:
- attn_heads: bfloat16 [8, 256, 2048], P('ep', None, 'dp'), may hold values from -6 to 6
- residual: bfloat16 [8, 256, 2048], P('ep', 'dp'), may hold values from -6 to 6
- w_out: bfloat16 [2048, 2048], P('dp'), may hold values from -0.125 to 0.125
- gain_post: bfloat16 [2048], replicated, may hold values from 0.5 to 1.5
- w_router: bfloat16 [2048, 60], replicated, may hold values from -0.125 to 0.125
- expert_ids: int32 [8, 256, 4], P('ep', 'dp'), may hold values from 0 to 59, all different within a row; in each aligned block of 64 rows (0 to 63, 64 to 127, ..., all dimensions but the last counted through in order) at most 8 rows name the same one
- expert_slot: int32 [60], replicated, may hold values from 0 to 63, as said below
- w_gate: bfloat16 [64, 2048, 1408], P('ep', None, 'dp'), may hold values from -0.125 to 0.125
- w_up: bfloat16 [64, 2048, 1408], P('ep', None, 'dp'), may hold values from -0.125 to 0.125
- w_down: bfloat16 [64, 1408, 2048], P('ep', 'dp'), may hold values from -0.15625 to 0.15625
- w_shared_gate: bfloat16 [2048, 5632], P(None, 'ep'), may hold values from -0.125 to 0.125
- w_shared_up: bfloat16 [2048, 5632], P(None, 'ep'), may hold values from -0.125 to 0.125
- w_shared_down: bfloat16 [5632, 2048], P('ep'), may hold values from -0.078125 to 0.078125
- w_shared_score: bfloat16 [2048], replicated, may hold values from -0.125 to 0.125
- gain_final: bfloat16 [2048], replicated, may hold values from 0.5 to 1.5
Outputs:
- mixed_out: bfloat16 [8, 256, 2048], P('ep', 'dp')
- final_out: bfloat16 [8, 256, 2048], P('ep', 'dp')
The draws below stay inside these ranges and needn't reach their ends.
Inputs may be any that keep to these rules, and one draw needn't show every extreme that they name: `expert_ids`: each row names 4 different experts. Within the 64 rows of one device no expert is named by more than 8 rows, and in some device one expert is named by exactly 8 rows. All entries differ; expert e uses entry expert_slot[e] of w_gate, w_up and w_down, and index i of ep holds positions i * 8 to (i + 1) * 8 - 1.
All inputs are finite; a program needn't handle non-finite values.
Results may differ from the reference program's by a relative error of at most 0.02.
Values may be sent and summed in bfloat16 or wider, within the bound.
A program may use at most 128 MiB of HBM per device.

```python
import math
import jax
import jax.numpy as jnp
import numpy as np
from jax import lax

D = 2048
FE = 1408
FS = 5632
EXPERTS = 60
TOP = 4
TOK_DEV = 64
MOST = 8
EXP_POS = 64
GROUPS = 8
ROWS_GROUP = 256
N_DP = 4
N_EP = 8


def draw_expert_slot(key, part):
    return jax.random.permutation(key, EXP_POS)[:EXPERTS].astype(jnp.int32)


def steps_of(stream_key, dims, shards, smallest, top_value):
    def one(dim, shards_of):
        draws = jax.random.uniform(jax.random.fold_in(jax.random.fold_in(stream_key, 6), dim), (shards_of,), jnp.float32, smallest / len(shards), top_value / len(shards))
        return jnp.repeat(jnp.exp(draws), dims[dim] // shards_of).reshape((-1,) + (1,) * (len(dims) - dim - 1))

    level = one(*shards[0])
    for cut in shards[1:]:
        level = level * one(*cut)
    return level


def deal_out(rng, own, number, rows, amount, top, reach, lean):
    order = jax.random.permutation(rng, amount)
    crowded, usual = portions_of(amount, rows * top, reach, lean, True), portions_of(amount, rows * top, reach, lean, False)
    places = jnp.arange(amount)

    def named(tallies, offset_by):
        used = int((tallies > 0).sum())
        fixed = max(1, used // 4)
        passed = fixed + (places - fixed + offset_by * (used - fixed)) % max(1, amount - fixed)
        return jnp.zeros((amount,), jnp.int32).at[order[jnp.where(places < fixed, places, passed)]].set(jnp.asarray(tallies, jnp.int32))

    tallies = jnp.where(number % 4 == 0, named(crowded, number // 4), named(usual, number - number // 4 - 1))
    mixed = jax.random.permutation(jax.random.fold_in(own, 3), amount)
    source_of, taker = mixed[0:amount // 2 * 2:2], mixed[1:amount // 2 * 2:2]
    room = jnp.minimum(tallies[source_of] - 1, reach - tallies[taker]) // 2
    room = jnp.where((source_of == order[0]) | (taker == order[0]) | (tallies[taker] == 0), 0, jnp.maximum(room, 0))
    passed = jax.random.randint(jax.random.fold_in(own, 4), (amount // 2,), 0, 1 << 20) % (room + 1)
    tallies = tallies.at[source_of].add(-passed).at[taker].add(passed)
    members = jnp.searchsorted(jnp.cumsum(tallies), jnp.arange(rows * top), side="right").astype(jnp.int32)
    table = members.reshape(top, rows).T
    table = table[jax.random.permutation(jax.random.fold_in(own, 1), rows)]
    offset_by = jax.random.randint(jax.random.fold_in(own, 2), (rows, 1), 0, top)
    return jnp.take_along_axis(table, (jnp.arange(top)[None, :] + offset_by) % top, axis=1)


def portions_of(count, total, reach, lean, full):
    portions = [(1 << 20) // math.isqrt(standing ** lean) + 1 for standing in range(1, count + 1)]
    largest = reach if full else min(reach, max(-(-total // count), total * portions[0] // sum(portions)))
    least = 1 if total - largest >= count - 1 else 0
    given, rest = [largest] + [least] * (count - 1), total - largest - least * (count - 1)
    while rest > 0:
        movable = [i for i in range(1, count) if given[i] < largest] or [i for i in range(1, count) if given[i] < reach]
        pool, remaining = sum([portions[i] for i in movable]), rest
        for i in movable:
            extra = min(reach - given[i], max(1, remaining * portions[i] // pool), rest)
            given[i] = given[i] + extra
            rest = rest - extra
    return np.array(given)


def normal_values(rng, dims, width, limit, split=(), held_as=jnp.bfloat16):
    entries = width * jax.random.normal(rng, dims, jnp.float32)
    if split:
        entries = entries * steps_of(rng, dims, split, -0.22, 0.18)
    return jnp.clip(entries, -limit, limit).astype(held_as)


def setup_inputs(seed: int = 0) -> dict:
    key_list = jax.random.split(jax.random.key(seed), 16)
    attn_heads = normal_values(key_list[0], (GROUPS, ROWS_GROUP, D), 1.0, 6.0, ((0, 8), (2, 4)))
    residual = normal_values(key_list[1], (GROUPS, ROWS_GROUP, D), 1.0, 6.0, ((0, 8), (1, 4)))
    w_out = normal_values(key_list[2], (D, D), D ** -0.5, 0.125, ((0, 4),))
    gain_post = jnp.clip(1.0 + 0.1 * jax.random.normal(key_list[3], (D,), jnp.float32), 0.5, 1.5).astype(jnp.bfloat16)
    w_router = normal_values(key_list[4], (D, EXPERTS), D ** -0.5, 0.125)
    expert_ids_keys = jax.random.split(jax.random.fold_in(key_list[5], 1), GROUPS * ROWS_GROUP // TOK_DEV)
    expert_ids_turns = jax.random.permutation(jax.random.fold_in(key_list[5], 3), GROUPS * ROWS_GROUP // TOK_DEV)
    expert_ids = jax.vmap(lambda own, number: deal_out(jax.random.fold_in(key_list[5], 2), own, number, TOK_DEV, EXPERTS, TOP, MOST, 2))(expert_ids_keys, expert_ids_turns).reshape((GROUPS, ROWS_GROUP, TOP))
    expert_slot = draw_expert_slot(jax.random.fold_in(key_list[15], 71), 0)
    w_gate = normal_values(key_list[7], (EXP_POS, D, FE), D ** -0.5, 0.125, ((0, 8), (2, 4)))
    w_up = normal_values(key_list[8], (EXP_POS, D, FE), D ** -0.5, 0.125, ((0, 8), (2, 4)))
    w_down = normal_values(key_list[9], (EXP_POS, FE, D), FE ** -0.5, 0.15625, ((0, 8), (1, 4)))
    w_shared_gate = normal_values(key_list[10], (D, FS), D ** -0.5, 0.125, ((1, 8),))
    w_shared_up = normal_values(key_list[11], (D, FS), D ** -0.5, 0.125, ((1, 8),))
    w_shared_down = normal_values(key_list[12], (FS, D), FS ** -0.5, 0.078125, ((0, 8),))
    w_shared_score = normal_values(key_list[13], (D,), D ** -0.5, 0.125)
    gain_final = jnp.clip(1.0 + 0.1 * jax.random.normal(key_list[14], (D,), jnp.float32), 0.5, 1.5).astype(jnp.bfloat16)
    return {"attn_heads": attn_heads, "residual": residual, "w_out": w_out, "gain_post": gain_post, "w_router": w_router, "expert_ids": expert_ids, "expert_slot": expert_slot, "w_gate": w_gate, "w_up": w_up, "w_down": w_down, "w_shared_gate": w_shared_gate, "w_shared_up": w_shared_up, "w_shared_down": w_shared_down, "w_shared_score": w_shared_score, "gain_final": gain_final}


eps_norm = 1e-06

def rms_scale(values_in, gain_vec):
    values = values_in.astype(jnp.float32)
    return values * lax.rsqrt(lax.optimization_barrier(jnp.mean(values * values, axis=-1, keepdims=True)) + eps_norm) * gain_vec.astype(jnp.float32)

def reference(attn_heads, residual, w_out, gain_post, w_router, expert_ids, expert_slot, w_gate, w_up, w_down, w_shared_gate, w_shared_up, w_shared_down, w_shared_score, gain_final):
    rows_total = GROUPS * ROWS_GROUP
    head_rows = attn_heads.reshape(rows_total, D)
    resid_rows = residual.reshape(rows_total, D)
    chosen = expert_ids.reshape(rows_total, TOP).astype(jnp.int32)
    projected = jnp.dot(head_rows, w_out, preferred_element_type=jnp.float32)
    hidden_state = (resid_rows.astype(jnp.float32) + projected).astype(jnp.bfloat16)
    normed = rms_scale(hidden_state, gain_post).astype(jnp.bfloat16)
    logits = jnp.dot(normed, w_router, preferred_element_type=jnp.float32)
    picked = jnp.take_along_axis(logits, chosen, axis=1)
    exp_logits = jnp.exp(picked)
    route_weights = (exp_logits / lax.optimization_barrier(jnp.sum(exp_logits, axis=1, keepdims=True))).astype(jnp.bfloat16)
    capacity = MOST * N_DP * N_EP
    flat_ids = chosen.reshape(-1)
    piece_width = FE // N_DP

    def one_expert(expert_num):
        matches = flat_ids == expert_num
        found = jnp.nonzero(matches, size=capacity, fill_value=0)[0].astype(jnp.int32)
        valid = jnp.arange(capacity, dtype=jnp.int32) < jnp.sum(matches.astype(jnp.int32))
        row_index = (found // TOP).astype(jnp.int32)
        inputs = normed[row_index]
        position = expert_slot[expert_num]
        gate_part = jnp.dot(inputs, w_gate[position], preferred_element_type=jnp.float32)
        up_part = jnp.dot(inputs, w_up[position], preferred_element_type=jnp.float32)
        hidden = (jax.nn.silu(gate_part) * up_part).astype(jnp.bfloat16)
        hidden_blocks = hidden.reshape(capacity, N_DP, piece_width).astype(jnp.float32)
        down_blocks = w_down[position].reshape(N_DP, piece_width, D).astype(jnp.float32)
        partials = jnp.einsum('cpf,pfd->pcd', hidden_blocks, down_blocks)
        rounded = lax.optimization_barrier(partials.astype(jnp.bfloat16))
        output = lax.optimization_barrier(jnp.sum(rounded.astype(jnp.float32), axis=0)).astype(jnp.bfloat16)
        target = jnp.where(valid, found, rows_total * TOP).astype(jnp.int32)
        return (output, target)
    outputs, targets = lax.map(one_expert, jnp.arange(EXPERTS, dtype=jnp.int32))
    expert_rows = jnp.zeros((rows_total * TOP, D), jnp.bfloat16)
    expert_rows = expert_rows.at[targets.reshape(-1)].set(outputs.reshape(-1, D), mode='drop')
    expert_rows = expert_rows.reshape(rows_total, TOP, D).astype(jnp.float32)
    routed = lax.optimization_barrier(jnp.sum(route_weights.astype(jnp.float32)[:, :, None] * expert_rows, axis=1))
    shared_gate_part = jnp.dot(normed, w_shared_gate, preferred_element_type=jnp.float32)
    shared_up_part = jnp.dot(normed, w_shared_up, preferred_element_type=jnp.float32)
    shared_hidden = (jax.nn.silu(shared_gate_part) * shared_up_part).astype(jnp.bfloat16)
    shared_width = FS // N_EP
    hidden_pieces = jnp.transpose(shared_hidden.reshape(rows_total, N_EP, shared_width), (1, 0, 2))
    down_pieces = w_shared_down.reshape(N_EP, shared_width, D)

    def add_piece(total, block):
        piece_rows, piece_down = block
        part = jnp.dot(piece_rows, piece_down, preferred_element_type=jnp.float32)
        rounded = lax.optimization_barrier(part.astype(jnp.bfloat16))
        return (total + rounded.astype(jnp.float32), None)
    shared_sum, unused = lax.scan(add_piece, jnp.zeros((rows_total, D), jnp.float32), (hidden_pieces, down_pieces))
    shared_score = jax.nn.sigmoid(jnp.dot(normed, w_shared_score, preferred_element_type=jnp.float32))
    mixed_out = (hidden_state.astype(jnp.float32) + shared_score[:, None] * shared_sum + routed).astype(jnp.bfloat16)
    final_out = rms_scale(mixed_out, gain_final).astype(jnp.bfloat16)
    return (mixed_out.reshape(GROUPS, ROWS_GROUP, D), final_out.reshape(GROUPS, ROWS_GROUP, D))
```

```python
import functools

import jax
import jax.numpy as jnp
from jax import lax
from jax.experimental import pallas as pl
from jax.experimental.pallas import tpu as pltpu
from jax.sharding import PartitionSpec as P

MOST = 8
N_DP = 4

eps_norm = 1e-06

f32 = jnp.float32
bf16 = jnp.bfloat16


def place(axes=("dp", "ep")):
    dp = lax.axis_index("dp")
    ep = lax.axis_index("ep")
    core = ep % 2
    z = ep // 2
    low = dp % 2
    high = dp // 2
    flip_low = 1 - 2 * low
    flip_high = 2 - 4 * high
    first = dp + (1 - core) * flip_low + core * flip_high
    second = dp + core * flip_low + (1 - core) * flip_high
    return dp, z, core, first, second, 3 - dp


def greet(z_count, dp, z, core):
    barrier = pltpu.get_barrier_semaphore()

    def hello(d, e):
        pl.semaphore_signal(barrier, inc=1, device_id={"dp": d, "ep": e})

    for k in range(1, N_DP):
        hello((dp + k) % N_DP, z * 2 + core)
    for k in range(1, z_count):
        hello(dp, ((z + k) % z_count) * 2 + core)
    hello(dp, z * 2 + 1 - core)
    pl.semaphore_wait(barrier, N_DP - 1 + z_count - 1 + 1)


def gather_kernel(
    z_count, tok, attn, w_out, residual, gain, rows, hidden,
    outbox, inbox, own,
    ps, pr, zs, zr, fs, fr, ss, sr, cs, cr, local,
):
    dp, z, core, first, second, far = place()
    greet(z_count, dp, z, core)

    def send(src, dst, s_sem, r_sem, d, e):
        return pltpu.make_async_remote_copy(
            src_ref=src, dst_ref=dst, send_sem=s_sem, recv_sem=r_sem,
            device_id={"dp": d, "ep": e},
        )

    me = z * 2 + core
    pending = []
    projections = []
    for k in (2, 1, 3):
        q = (dp + k) % N_DP
        outbox[k - 1] = jnp.dot(
            attn[pl.ds(pl.multiple_of(q * tok, tok), tok), :], w_out[...],
            preferred_element_type=f32,
        ).astype(bf16)
        copy = send(outbox.at[k - 1], inbox.at[k - 1], ps.at[k - 1], pr.at[k - 1], q, me)
        copy.start()
        projections.append((k, copy))
    total = residual[...].astype(f32) + jnp.dot(
        attn[pl.ds(pl.multiple_of(dp * tok, tok), tok), :], w_out[...],
        preferred_element_type=f32,
    )
    for k, copy in projections:
        copy.wait_recv()
        total = total + inbox[k - 1].astype(f32)
    state = total.astype(bf16)
    hidden[...] = state
    wide = state.astype(f32)
    own[...] = (
        wide * lax.rsqrt(jnp.mean(wide * wide, axis=-1, keepdims=True) + eps_norm)
        * gain[...].astype(f32)
    ).astype(bf16)
    for k, copy in projections:
        copy.wait_send()

    def block(k, c, d):
        return rows.at[(((z + z_count - k) % z_count) * 2 + c) * N_DP + d]

    keep = pltpu.make_async_copy(own, block(0, core, dp), local.at[0])
    keep.start()

    def over_first(k):
        src = own if k == 0 else block(k, core, dp)
        return send(src, block(k, core, dp), fs.at[k], fr.at[k], first, me)

    def over_second(k, j):
        d = dp if j == 0 else first
        src = own if k == 0 and j == 0 else block(k, core, d)
        return send(src, block(k, core, d), ss.at[2 * k + j], sr.at[2 * k + j], second, me)

    def over_core(k, j):
        d = (dp, first, second, far)[j]
        src = own if k == 0 and j == 0 else block(k, core, d)
        return send(src, block(k, core, d), cs.at[4 * k + j], cr.at[4 * k + j], dp, z * 2 + 1 - core)

    def arrived(sem, ref):
        pltpu.make_async_copy(ref, ref, sem).wait()

    def go(copy):
        copy.start()
        pending.append(copy)

    go(over_first(0))
    go(over_second(0, 0))
    for k in range(1, z_count):
        go(send(own, block(0, core, dp), zs.at[k], zr.at[k], dp, ((z + k) % z_count) * 2 + core))
    go(over_core(0, 0))

    def tail(k):
        for j, d in ((0, second), (1, far)):
            arrived(sr.at[2 * k + j], block(k, core, d))
            go(over_core(k, 2 + j))

    for k in range(z_count):
        if k > 0:
            arrived(zr.at[k], block(k, core, dp))
            go(over_first(k))
            go(over_second(k, 0))
            go(over_core(k, 0))
        arrived(fr.at[k], block(k, core, first))
        go(over_second(k, 1))
        go(over_core(k, 1))
        if k > 0:
            tail(k - 1)
    tail(z_count - 1)
    for k in range(z_count):
        for j, d in ((0, dp), (1, second), (2, first), (3, far)):
            arrived(cr.at[4 * k + j], block(k, 1 - core, d))
    for copy in pending:
        copy.wait_send()
    keep.wait()


def project_and_gather(z_count, attn, w_out, residual, gain):
    tok, width = residual.shape
    count = z_count * 2 * N_DP
    dma = pltpu.SemaphoreType.DMA
    vmem = pl.BlockSpec(memory_space=pltpu.VMEM)
    return pl.pallas_call(
        functools.partial(gather_kernel, z_count, tok),
        out_shape=(
            jax.ShapeDtypeStruct((count, tok, width), bf16),
            jax.ShapeDtypeStruct((tok, width), bf16),
        ),
        in_specs=[vmem] * 4,
        out_specs=(pl.BlockSpec(memory_space=pl.ANY), vmem),
        scratch_shapes=[
            pltpu.VMEM((N_DP - 1, tok, width), bf16),
            pltpu.VMEM((N_DP - 1, tok, width), bf16),
            pltpu.VMEM((tok, width), bf16),
            dma((N_DP - 1,)), dma((N_DP - 1,)),
            dma((z_count,)), dma((z_count,)),
            dma((z_count,)), dma((z_count,)),
            dma((2 * z_count,)), dma((2 * z_count,)),
            dma((4 * z_count,)), dma((4 * z_count,)),
            dma((1,)),
        ],
        compiler_params=pltpu.CompilerParams(
            collective_id=0, has_side_effects=True, vmem_limit_bytes=32 << 20
        ),
        name="project_gather",
    )(attn, w_out, residual, gain)


def scatter_kernel(
    z_count, part, hidden, gain, mixed, final,
    acc, from_core, from_second, from_first, from_z,
    cs, cr, ss, sr, fs, fr, zs, zr, local,
):
    dp, z, core, first, second, far = place()
    greet(z_count, dp, z, core)
    me = z * 2 + core
    dest = (dp, first, second, far)
    pending = []
    order = list(range(1, z_count)) + [0]

    def send(src, dst, s_sem, r_sem, d, e):
        copy = pltpu.make_async_remote_copy(
            src_ref=src, dst_ref=dst, send_sem=s_sem, recv_sem=r_sem,
            device_id={"dp": d, "ep": e},
        )
        copy.start()
        pending.append(copy)

    def level(k):
        return (z + z_count - k) % z_count

    def arrived(sem, ref):
        pltpu.make_async_copy(ref, ref, sem).wait()

    def begin(k, j):
        i = 4 * k + j
        there = (dp, second, first, far)[j]
        pltpu.make_async_copy(
            part.at[(level(k) * 2 + core) * N_DP + dest[j]], acc.at[i], local.at[i]
        ).start()
        send(
            part.at[(level(k) * 2 + 1 - core) * N_DP + there], from_core.at[i],
            cs.at[i], cr.at[i], dp, z * 2 + 1 - core,
        )

    for j in (3, 2, 1, 0):
        for k in order:
            begin(k, j)

    def pair(k, j):
        i = 4 * k + j
        arrived(local.at[i], acc.at[i])
        arrived(cr.at[i], from_core.at[i])
        return acc[i].astype(f32) + from_core[i].astype(f32)

    for j in (3, 2):
        for k in order:
            acc[4 * k + j] = pair(k, j).astype(bf16)
            i = 2 * k + j - 2
            send(acc.at[4 * k + j], from_second.at[i], ss.at[i], sr.at[i], second, me)

    def summed(k, j):
        i = 2 * k + j
        value = pair(k, j)
        arrived(sr.at[i], from_second.at[i])
        return value + from_second[i].astype(f32)

    def pass_first(k):
        acc[4 * k + 1] = summed(k, 1).astype(bf16)
        send(acc.at[4 * k + 1], from_first.at[k], fs.at[k], fr.at[k], first, me)

    def pass_z(k):
        value = summed(k, 0)
        arrived(fr.at[k], from_first.at[k])
        value = value + from_first[k].astype(f32)
        if k > 0:
            acc[4 * k] = value.astype(bf16)
            send(acc.at[4 * k], from_z.at[k], zs.at[k], zr.at[k], dp, level(k) * 2 + core)
            return None
        return value

    for k in order:
        pass_first(k)
    for k in order:
        value = pass_z(k)
    for k in range(1, z_count):
        arrived(zr.at[k], from_z.at[k])
        value = value + from_z[k].astype(f32)
    out = (hidden[...].astype(f32) + value).astype(bf16)
    mixed[...] = out
    wide = out.astype(f32)
    final[...] = (
        wide * lax.rsqrt(jnp.mean(wide * wide, axis=-1, keepdims=True) + eps_norm)
        * gain[...].astype(f32)
    ).astype(bf16)
    for copy in pending:
        copy.wait_send()


def reduce_and_norm(z_count, part, hidden, gain):
    tok, width = hidden.shape
    dma = pltpu.SemaphoreType.DMA
    vmem = pl.BlockSpec(memory_space=pltpu.VMEM)
    shape = jax.ShapeDtypeStruct((tok, width), bf16)
    boxes = [4 * z_count, 4 * z_count, 2 * z_count, z_count, z_count]
    sems = [4 * z_count] * 2 + [2 * z_count] * 2 + [z_count] * 4 + [4 * z_count]
    return pl.pallas_call(
        functools.partial(scatter_kernel, z_count),
        out_shape=(shape, shape),
        in_specs=[pl.BlockSpec(memory_space=pl.ANY), vmem, vmem],
        out_specs=(vmem, vmem),
        scratch_shapes=[pltpu.VMEM((n, tok, width), bf16) for n in boxes]
        + [dma((n,)) for n in sems],
        compiler_params=pltpu.CompilerParams(
            collective_id=1, has_side_effects=True, vmem_limit_bytes=56 << 20
        ),
        name="reduce_norm",
    )(part, hidden, gain)


def expert_kernel(
    groups, experts, tok, where_ref, x_ref, send_ref, gate_ref, up_ref, down_ref, back_ref, shared_ref,
    out_ref, cells, results,
):
    step = pl.program_id(0)
    wide = N_DP * MOST

    @pl.when(step < groups)
    def _():
        picked = jnp.dot(send_ref[0], x_ref[0], preferred_element_type=f32).astype(bf16)
        for e in range(experts):
            cells[e, pl.ds(pl.multiple_of(step * wide, wide), wide), :] = picked[e * wide:(e + 1) * wide]

    @pl.when((step >= groups) & (step < groups + experts))
    def _():
        e = step - groups
        rows = cells[e]
        gate = jnp.dot(rows, gate_ref[0], preferred_element_type=f32)
        up = jnp.dot(rows, up_ref[0], preferred_element_type=f32)
        hidden = (gate / (1.0 + jnp.exp(-gate)) * up).astype(bf16)
        result = jnp.dot(hidden, down_ref[0], preferred_element_type=f32).astype(bf16)
        for g in range(groups):
            results[g, pl.ds(pl.multiple_of(e * wide, wide), wide), :] = result[g * wide:(g + 1) * wide]

    @pl.when(step >= groups + experts)
    def _():
        g = step - groups - experts
        out_ref[0] = jnp.dot(back_ref[0], results[g], preferred_element_type=f32).astype(bf16)
        mine = pl.ds(pl.multiple_of(where_ref[0] * tok, tok), tok)
        out_ref[0, mine, :] = (out_ref[0, mine, :].astype(f32) + shared_ref[0].astype(f32)).astype(bf16)


def run_experts(x, send_mat, back_mat, w_gate, w_up, w_down, shared):
    groups, rows, width = x.shape
    experts, _, units = w_gate.shape
    cells = send_mat.shape[1]
    tok = rows // N_DP
    per_expert = groups * N_DP * MOST

    def at_group(i, *_):
        return (jnp.minimum(i, groups - 1), 0, 0)

    def at_expert(i, *_):
        return (jnp.clip(i - groups, 0, experts - 1), 0, 0)

    def at_end(i, *_):
        return (jnp.clip(i - groups - experts, 0, groups - 1), 0, 0)

    return pl.pallas_call(
        functools.partial(expert_kernel, groups, experts, tok),
        out_shape=jax.ShapeDtypeStruct((groups, rows, width), bf16),
        grid_spec=pltpu.PrefetchScalarGridSpec(
            num_scalar_prefetch=1,
            grid=(2 * groups + experts,),
            in_specs=[
                pl.BlockSpec((1, rows, width), at_group),
                pl.BlockSpec((1, cells, rows), at_group),
                pl.BlockSpec((1, width, units), at_expert),
                pl.BlockSpec((1, width, units), at_expert),
                pl.BlockSpec((1, units, width), at_expert),
                pl.BlockSpec((1, rows, cells), at_end),
                pl.BlockSpec((1, tok, width), at_end),
            ],
            out_specs=pl.BlockSpec((1, rows, width), at_end),
            scratch_shapes=[
                pltpu.VMEM((experts, per_expert, width), bf16),
                pltpu.VMEM((groups, cells, width), bf16),
            ],
        ),
        compiler_params=pltpu.CompilerParams(vmem_limit_bytes=56 << 20),
        name="experts",
    )(lax.axis_index("dp").astype(jnp.int32).reshape(1), x, send_mat, w_gate, w_up, w_down, back_mat, shared)


def per_device(
    attn_heads,
    residual,
    w_out,
    gain_post,
    w_router,
    expert_ids,
    expert_slot,
    w_gate,
    w_up,
    w_down,
    w_shared_gate,
    w_shared_up,
    w_shared_down,
    w_shared_score,
    gain_final,
):
    groups = lax.axis_size("ep")
    z_count = groups // 2
    experts_here = w_gate.shape[0]
    expert_count = w_router.shape[1]
    width = residual.shape[2]
    tok = residual.shape[1]
    rows = N_DP * tok
    spread = N_DP * MOST

    ids = lax.all_gather(expert_ids[0], ("ep", "dp"), axis=0, tiled=False)
    ids = ids.reshape(groups * N_DP, tok, -1)
    names = ids[..., None] == jnp.arange(expert_count, dtype=jnp.int32)
    chosen = jnp.any(names, axis=2)
    here = lax.axis_index("ep") * experts_here + jnp.arange(experts_here, dtype=jnp.int32)
    local = (expert_slot[:, None] == here[None, :]).astype(f32)
    hits = jnp.einsum("stx,xe->ste", chosen.astype(bf16), local.astype(bf16), preferred_element_type=f32)
    below = jnp.tril(jnp.ones((tok, tok), bf16), -1)
    rank = jnp.einsum("ut,ste->sue", below, hits.astype(bf16), preferred_element_type=f32)
    part = (jnp.arange(groups * N_DP, dtype=jnp.int32) % N_DP * MOST)[:, None, None]
    cell = jnp.where(hits > 0.5, rank.astype(jnp.int32) + part, -1).reshape(groups, rows, experts_here)
    numbers = jnp.arange(spread, dtype=jnp.int32)
    send_mat = (jnp.swapaxes(cell, 1, 2)[:, :, None, :] == numbers[None, None, :, None]).astype(bf16)
    send_mat = send_mat.reshape(groups, experts_here * spread, rows)

    x_all, hidden_state = project_and_gather(
        z_count, attn_heads[0], w_out, residual[0], gain_post.reshape(1, width)
    )
    x = x_all.reshape(groups, rows, width)

    logits = jnp.einsum("grd,dx->grx", x, w_router, preferred_element_type=f32)
    powers = jnp.where(chosen.reshape(groups, rows, expert_count), jnp.exp(logits), 0.0)
    weights = powers / jnp.sum(powers, axis=-1, keepdims=True)
    mine = jnp.einsum("grx,xe->gre", weights.astype(bf16), local.astype(bf16), preferred_element_type=f32)
    back_mat = jnp.where(cell[:, :, :, None] == numbers, mine[:, :, :, None], 0.0)
    back_mat = back_mat.astype(bf16).reshape(groups, rows, experts_here * spread)

    line = lax.dynamic_index_in_dim(
        x.reshape(groups, N_DP, tok, width), lax.axis_index("dp"), axis=1, keepdims=False
    ).reshape(groups * tok, width)
    gate_part = jnp.dot(line, w_shared_gate, preferred_element_type=f32)
    up_part = jnp.dot(line, w_shared_up, preferred_element_type=f32)
    shared_hidden = (jax.nn.silu(gate_part) * up_part).astype(bf16)
    score = jax.nn.sigmoid(jnp.dot(line, w_shared_score, preferred_element_type=f32))
    shared = (
        jnp.dot(shared_hidden, w_shared_down, preferred_element_type=f32) * score[:, None]
    ).astype(bf16).reshape(groups, tok, width)

    partial_sums = run_experts(x, send_mat, back_mat, w_gate, w_up, w_down, shared)
    mixed_out, final_out = reduce_and_norm(
        z_count, partial_sums.reshape(groups * N_DP, tok, width), hidden_state,
        gain_final.reshape(1, width),
    )
    return (mixed_out[None], final_out[None])


def solution(mesh):
    in_specs = (
        P("ep", None, "dp"),
        P("ep", "dp", None),
        P("dp", None),
        P(),
        P(),
        P("ep", "dp", None),
        P(),
        P("ep", None, "dp"),
        P("ep", None, "dp"),
        P("ep", "dp", None),
        P(None, "ep"),
        P(None, "ep"),
        P("ep", None),
        P(),
        P(),
    )
    out_specs = (P("ep", "dp", None), P("ep", "dp", None))
    return jax.shard_map(
        per_device, mesh=mesh, in_specs=in_specs, out_specs=out_specs, check_vma=False
    )
```

```python
import functools

import jax
import jax.numpy as jnp
import numpy as np
from jax import lax
from jax.experimental import pallas as pl
from jax.experimental.pallas import tpu as pltpu
from jax.sharding import PartitionSpec as P

MOST = 8
N_DP = 4

eps_norm = 1e-06

f32 = jnp.float32
bf16 = jnp.bfloat16


def place(axes=("dp", "ep")):
    dp = lax.axis_index("dp")
    ep = lax.axis_index("ep")
    core = ep % 2
    z = ep // 2
    low = dp % 2
    high = dp // 2
    flip_low = 1 - 2 * low
    flip_high = 2 - 4 * high
    first = dp + (1 - core) * flip_low + core * flip_high
    second = dp + core * flip_low + (1 - core) * flip_high
    return dp, z, core, first, second, 3 - dp


def greet(z_count, dp, z, core):
    barrier = pltpu.get_barrier_semaphore()

    def hello(d, e):
        pl.semaphore_signal(barrier, inc=1, device_id={"dp": d, "ep": e})

    for k in range(1, N_DP):
        hello((dp + k) % N_DP, z * 2 + core)
    for k in range(1, z_count):
        hello(dp, ((z + k) % z_count) * 2 + core)
    hello(dp, z * 2 + 1 - core)
    pl.semaphore_wait(barrier, N_DP - 1 + z_count - 1 + 1)


def rows_dot(a, b):
    return lax.dot_general(a, b, (((1,), (1,)), ((), ())), preferred_element_type=f32)


def gather_kernel(
    z_count, tok, attn, w_out, residual, gain, ids, gate_hbm, up_hbm, down_hbm,
    rows, hidden, ids_out, shared,
    outbox, inbox, own, names, gate_w, up_w, down_w, line,
    ps, pr, zs, zr, fs, fr, ss, sr, cs, cr, local, weight_sem, line_sem,
    izs, izr, ifs, ifr, iss, isr, ics, icr,
):
    dp, z, core, first, second, far = place()
    greet(z_count, dp, z, core)

    def send(src, dst, s_sem, r_sem, d, e):
        return pltpu.make_async_remote_copy(
            src_ref=src, dst_ref=dst, send_sem=s_sem, recv_sem=r_sem,
            device_id={"dp": d, "ep": e},
        )

    me = z * 2 + core
    pending = []
    projections = []
    loads = [
        pltpu.make_async_copy(src, dst, weight_sem.at[i])
        for i, (src, dst) in enumerate(((gate_hbm, gate_w), (up_hbm, up_w), (down_hbm, down_w)))
    ]
    for load in loads:
        load.start()

    def arrived(sem, ref):
        pltpu.make_async_copy(ref, ref, sem).wait()

    def go(copy):
        copy.start()
        pending.append(copy)

    names[core, dp, z] = ids[...]
    for k in range(1, z_count):
        spot = names.at[core, dp, z]
        go(send(spot, spot, izs.at[k], izr.at[k], dp, ((z + k) % z_count) * 2 + core))

    def names_step(step):
        if step == 0:
            for k in range(1, z_count):
                arrived(izr.at[k], names.at[core, dp, (z + z_count - k) % z_count])
            spot = names.at[core, dp]
            go(send(spot, spot, ifs.at[0], ifr.at[0], first, me))
        elif step == 1:
            arrived(ifr.at[0], names.at[core, first])
            for i, d in ((0, dp), (1, first)):
                spot = names.at[core, d]
                go(send(spot, spot, iss.at[i], isr.at[i], second, me))
        elif step == 2:
            arrived(isr.at[0], names.at[core, second])
            arrived(isr.at[1], names.at[core, far])
            spot = names.at[core]
            go(send(spot, spot, ics.at[0], icr.at[0], dp, z * 2 + 1 - core))

    for step, k in enumerate((2, 1, 3)):
        q = (dp + k) % N_DP
        outbox[k - 1] = jnp.dot(
            attn[pl.ds(pl.multiple_of(q * tok, tok), tok), :], w_out[...],
            preferred_element_type=f32,
        ).astype(bf16)
        copy = send(outbox.at[k - 1], inbox.at[k - 1], ps.at[k - 1], pr.at[k - 1], q, me)
        copy.start()
        projections.append((k, copy))
        names_step(step)
    total = residual[...].astype(f32) + jnp.dot(
        attn[pl.ds(pl.multiple_of(dp * tok, tok), tok), :], w_out[...],
        preferred_element_type=f32,
    )
    for k, copy in projections:
        copy.wait_recv()
        total = total + inbox[k - 1].astype(f32)
    state = total.astype(bf16)
    hidden[...] = state
    wide = state.astype(f32)
    own[...] = (
        wide * lax.rsqrt(jnp.mean(wide * wide, axis=-1, keepdims=True) + eps_norm)
        * gain[...].astype(f32)
    ).astype(bf16)
    for k, copy in projections:
        copy.wait_send()

    def block(k, c, d):
        return rows.at[(((z + z_count - k) % z_count) * 2 + c) * N_DP + d]

    keep = pltpu.make_async_copy(own, block(0, core, dp), local.at[0])
    keep.start()

    def over_first(k):
        src = own if k == 0 else block(k, core, dp)
        return send(src, block(k, core, dp), fs.at[k], fr.at[k], first, me)

    def over_second(k, j):
        d = dp if j == 0 else first
        src = own if k == 0 and j == 0 else block(k, core, d)
        return send(src, block(k, core, d), ss.at[2 * k + j], sr.at[2 * k + j], second, me)

    def over_core(k, j):
        d = (dp, first, second, far)[j]
        src = own if k == 0 and j == 0 else block(k, core, d)
        return send(src, block(k, core, d), cs.at[4 * k + j], cr.at[4 * k + j], dp, z * 2 + 1 - core)

    def share(c):
        for start in range(0, z_count, 4):
            some = range(start, min(start + 4, z_count))
            moves = []
            for i, k in enumerate(some):
                if c == 1:
                    arrived(cr.at[4 * k], block(k, 1 - core, dp))
                elif k == 0:
                    keep.wait()
                where = block(k, core if c == 0 else 1 - core, dp)
                move = pltpu.make_async_copy(where, line.at[pl.ds(i * tok, tok)], line_sem.at[i])
                move.start()
                moves.append(move)
            for move in moves:
                move.wait()
            count = len(moves) * tok
            x = line[:count]
            gate = rows_dot(x, gate_w[...])
            up = rows_dot(x, up_w[...])
            units = (gate / (1.0 + jnp.exp(-gate)) * up).astype(bf16)
            out = jnp.dot(units, down_w[...], preferred_element_type=f32).astype(bf16)
            for i, k in enumerate(some):
                level = (z + z_count - k) % z_count
                shared[level * 2 + (core if c == 0 else 1 - core)] = out[i * tok:(i + 1) * tok]

    go(over_first(0))
    go(over_second(0, 0))
    for k in range(1, z_count):
        go(send(own, block(0, core, dp), zs.at[k], zr.at[k], dp, ((z + k) % z_count) * 2 + core))
    go(over_core(0, 0))

    def tail(k):
        for j, d in ((0, second), (1, far)):
            arrived(sr.at[2 * k + j], block(k, core, d))
            go(over_core(k, 2 + j))

    for k in range(z_count):
        if k > 0:
            arrived(zr.at[k], block(k, core, dp))
            go(over_first(k))
            go(over_second(k, 0))
            go(over_core(k, 0))
        arrived(fr.at[k], block(k, core, first))
        go(over_second(k, 1))
        go(over_core(k, 1))
        if k == z_count - 1:
            for load in loads:
                load.wait()
            share(0)
        if k > 0:
            tail(k - 1)
    share(1)
    tail(z_count - 1)
    arrived(icr.at[0], names.at[1 - core])
    for c in range(2):
        for d in range(N_DP):
            for level in range(z_count):
                ids_out[level * 2 + c, :, d * tok:(d + 1) * tok] = names[c, d, level][:, :tok]
    for k in range(z_count):
        for j, d in ((1, second), (2, first), (3, far)):
            arrived(cr.at[4 * k + j], block(k, 1 - core, d))
    for copy in pending:
        copy.wait_send()


def project_and_gather(z_count, attn, w_out, residual, gain, ids, gate, up, down):
    units = down.shape[0]
    tok, width = residual.shape
    count = z_count * 2 * N_DP
    dma = pltpu.SemaphoreType.DMA
    vmem = pl.BlockSpec(memory_space=pltpu.VMEM)
    return pl.pallas_call(
        functools.partial(gather_kernel, z_count, tok),
        out_shape=(
            jax.ShapeDtypeStruct((count, tok, width), bf16),
            jax.ShapeDtypeStruct((tok, width), bf16),
            jax.ShapeDtypeStruct((z_count * 2, 8, N_DP * tok), jnp.int32),
            jax.ShapeDtypeStruct((z_count * 2, tok, width), bf16),
        ),
        in_specs=[vmem] * 5 + [pl.BlockSpec(memory_space=pl.ANY)] * 3,
        out_specs=(pl.BlockSpec(memory_space=pl.ANY), vmem, vmem, vmem),
        scratch_shapes=[
            pltpu.VMEM((N_DP - 1, tok, width), bf16),
            pltpu.VMEM((N_DP - 1, tok, width), bf16),
            pltpu.VMEM((tok, width), bf16),
            pltpu.VMEM((2, N_DP, z_count, 8, 128), jnp.int32),
            pltpu.VMEM((units, width), bf16),
            pltpu.VMEM((units, width), bf16),
            pltpu.VMEM((units, width), bf16),
            pltpu.VMEM((4 * tok, width), bf16),
            dma((N_DP - 1,)), dma((N_DP - 1,)),
            dma((z_count,)), dma((z_count,)),
            dma((z_count,)), dma((z_count,)),
            dma((2 * z_count,)), dma((2 * z_count,)),
            dma((4 * z_count,)), dma((4 * z_count,)),
            dma((1,)), dma((3,)), dma((4,)),
            dma((z_count,)), dma((z_count,)),
            dma((1,)), dma((1,)),
            dma((2,)), dma((2,)),
            dma((1,)), dma((1,)),
        ],
        compiler_params=pltpu.CompilerParams(
            collective_id=0, has_side_effects=True, vmem_limit_bytes=48 << 20
        ),
        name="project_gather",
    )(attn, w_out, residual, gain, ids, gate, up, down)


def scatter_kernel(
    z_count, part, hidden, gain, mixed, final,
    acc, from_core, from_second, from_first, from_z,
    cs, cr, ss, sr, fs, fr, zs, zr, local,
):
    dp, z, core, first, second, far = place()
    greet(z_count, dp, z, core)
    me = z * 2 + core
    dest = (dp, first, second, far)
    pending = []
    order = list(range(1, z_count)) + [0]

    def send(src, dst, s_sem, r_sem, d, e):
        copy = pltpu.make_async_remote_copy(
            src_ref=src, dst_ref=dst, send_sem=s_sem, recv_sem=r_sem,
            device_id={"dp": d, "ep": e},
        )
        copy.start()
        pending.append(copy)

    def level(k):
        return (z + z_count - k) % z_count

    def arrived(sem, ref):
        pltpu.make_async_copy(ref, ref, sem).wait()

    def begin(k, j):
        i = 4 * k + j
        there = (dp, second, first, far)[j]
        pltpu.make_async_copy(
            part.at[(level(k) * 2 + core) * N_DP + dest[j]], acc.at[i], local.at[i]
        ).start()
        send(
            part.at[(level(k) * 2 + 1 - core) * N_DP + there], from_core.at[i],
            cs.at[i], cr.at[i], dp, z * 2 + 1 - core,
        )

    for j in (3, 2, 1, 0):
        for k in order:
            begin(k, j)

    def pair(k, j):
        i = 4 * k + j
        arrived(local.at[i], acc.at[i])
        arrived(cr.at[i], from_core.at[i])
        return acc[i].astype(f32) + from_core[i].astype(f32)

    for j in (3, 2):
        for k in order:
            acc[4 * k + j] = pair(k, j).astype(bf16)
            i = 2 * k + j - 2
            send(acc.at[4 * k + j], from_second.at[i], ss.at[i], sr.at[i], second, me)

    def summed(k, j):
        i = 2 * k + j
        value = pair(k, j)
        arrived(sr.at[i], from_second.at[i])
        return value + from_second[i].astype(f32)

    def pass_first(k):
        acc[4 * k + 1] = summed(k, 1).astype(bf16)
        send(acc.at[4 * k + 1], from_first.at[k], fs.at[k], fr.at[k], first, me)

    def pass_z(k):
        value = summed(k, 0)
        arrived(fr.at[k], from_first.at[k])
        value = value + from_first[k].astype(f32)
        if k > 0:
            acc[4 * k] = value.astype(bf16)
            send(acc.at[4 * k], from_z.at[k], zs.at[k], zr.at[k], dp, level(k) * 2 + core)
            return None
        return value

    for k in order:
        pass_first(k)
    for k in order:
        value = pass_z(k)
    for k in range(1, z_count):
        arrived(zr.at[k], from_z.at[k])
        value = value + from_z[k].astype(f32)
    out = (hidden[...].astype(f32) + value).astype(bf16)
    mixed[...] = out
    wide = out.astype(f32)
    final[...] = (
        wide * lax.rsqrt(jnp.mean(wide * wide, axis=-1, keepdims=True) + eps_norm)
        * gain[...].astype(f32)
    ).astype(bf16)
    for copy in pending:
        copy.wait_send()


def reduce_and_norm(z_count, part, hidden, gain):
    tok, width = hidden.shape
    dma = pltpu.SemaphoreType.DMA
    vmem = pl.BlockSpec(memory_space=pltpu.VMEM)
    shape = jax.ShapeDtypeStruct((tok, width), bf16)
    boxes = [4 * z_count, 4 * z_count, 2 * z_count, z_count, z_count]
    sems = [4 * z_count] * 2 + [2 * z_count] * 2 + [z_count] * 4 + [4 * z_count]
    return pl.pallas_call(
        functools.partial(scatter_kernel, z_count),
        out_shape=(shape, shape),
        in_specs=[pl.BlockSpec(memory_space=pl.ANY), vmem, vmem],
        out_specs=(vmem, vmem),
        scratch_shapes=[pltpu.VMEM((n, tok, width), bf16) for n in boxes]
        + [dma((n,)) for n in sems],
        compiler_params=pltpu.CompilerParams(
            collective_id=1, has_side_effects=True, vmem_limit_bytes=56 << 20
        ),
        name="reduce_norm",
    )(part, hidden, gain)


def expert_kernel(
    groups, experts, tok, where_ref, x_ref, ids_ref, router_ref, cell_expert_ref, cell_number_ref,
    before_ref, source_ref, gate_ref, up_ref, down_ref, shared_ref,
    out_ref, cells, results, back, logits_ref,
):
    step = pl.program_id(0)
    wide = N_DP * MOST

    @pl.when(step < groups)
    def _():
        x = x_ref[0]
        logits = rows_dot(x, router_ref[...])
        logits_ref[step] = logits
        lined = logits.T
        numbers = lax.broadcasted_iota(jnp.int32, lined.shape, 0)
        chosen = numbers == ids_ref[0, 0:1, :]
        for k in range(1, 4):
            chosen = chosen | (numbers == ids_ref[0, k:k + 1, :])
        powers = jnp.where(chosen, jnp.exp(lined), 0.0)
        weights = (powers / jnp.sum(powers, axis=0, keepdims=True)).astype(bf16)
        hit = jnp.where(chosen, 1.0, 0.0).astype(bf16)
        rank = jnp.dot(hit, before_ref[...], preferred_element_type=f32) + source_ref[...]
        at_cell = cell_expert_ref[...]
        named = jnp.dot(at_cell, hit, preferred_element_type=f32)
        spot = jnp.dot(at_cell, rank.astype(bf16), preferred_element_type=f32)
        weight = jnp.dot(at_cell, weights, preferred_element_type=f32)
        here = (named > 0.5) & (spot == cell_number_ref[...])
        back[step] = jnp.where(here, weight, 0.0).T.astype(bf16)
        picked = jnp.dot(
            jnp.where(here, 1.0, 0.0).astype(bf16), x, preferred_element_type=f32
        ).astype(bf16)
        for e in range(experts):
            cells[e, pl.ds(pl.multiple_of(step * wide, wide), wide), :] = picked[e * wide:(e + 1) * wide]

    @pl.when((step >= groups) & (step < groups + experts))
    def _():
        e = step - groups
        rows = cells[e]
        gate = rows_dot(rows, gate_ref[0])
        up = rows_dot(rows, up_ref[0])
        hidden = (gate / (1.0 + jnp.exp(-gate)) * up).astype(bf16)
        result = jnp.dot(hidden, down_ref[0], preferred_element_type=f32).astype(bf16)
        for g in range(groups):
            results[g, pl.ds(pl.multiple_of(e * wide, wide), wide), :] = result[g * wide:(g + 1) * wide]

    @pl.when(step >= groups + experts)
    def _():
        g = step - groups - experts
        out_ref[0] = jnp.dot(back[g], results[g], preferred_element_type=f32).astype(bf16)
        mine = pl.ds(pl.multiple_of(where_ref[0] * tok, tok), tok)
        last = where_ref[1]
        columns = logits_ref[g, mine, :]
        lane = lax.broadcasted_iota(jnp.int32, columns.shape, 1)
        score = jnp.sum(jnp.where(lane == last, columns, 0.0), axis=1, keepdims=True)
        score = 1.0 / (1.0 + jnp.exp(-score))
        out_ref[0, mine, :] = (
            out_ref[0, mine, :].astype(f32) + score * shared_ref[0].astype(f32)
        ).astype(bf16)


def run_experts(x, ids, router, cell_expert, score_row, w_gate, w_up, w_down, shared):
    groups, rows, width = x.shape
    experts, units, _ = w_gate.shape
    cells, known = cell_expert.shape
    tok = rows // N_DP
    spread = N_DP * MOST
    place_of = np.arange(rows)
    before = (place_of[:, None] < place_of[None, :]) & (
        place_of[:, None] // tok == place_of[None, :] // tok
    )
    before = jnp.asarray(before, bf16)
    source = jnp.asarray(place_of[None, :] // tok * MOST, f32)
    cell_number = jnp.asarray(np.arange(cells)[:, None] % spread, f32)

    def at_group(i, *_):
        return (jnp.minimum(i, groups - 1), 0, 0)

    def at_expert(i, *_):
        return (jnp.clip(i - groups, 0, experts - 1), 0, 0)

    def at_end(i, *_):
        return (jnp.clip(i - groups - experts, 0, groups - 1), 0, 0)

    def whole(i, *_):
        return (0, 0)

    where = jnp.stack([lax.axis_index("dp").astype(jnp.int32), jnp.int32(score_row)])
    return pl.pallas_call(
        functools.partial(expert_kernel, groups, experts, tok),
        out_shape=jax.ShapeDtypeStruct((groups, rows, width), bf16),
        grid_spec=pltpu.PrefetchScalarGridSpec(
            num_scalar_prefetch=1,
            grid=(2 * groups + experts,),
            in_specs=[
                pl.BlockSpec((1, rows, width), at_group),
                pl.BlockSpec((1, 8, rows), at_group),
                pl.BlockSpec(router.shape, whole),
                pl.BlockSpec((cells, known), whole),
                pl.BlockSpec((cells, 1), whole),
                pl.BlockSpec((rows, rows), whole),
                pl.BlockSpec((1, rows), whole),
                pl.BlockSpec((1, units, width), at_expert),
                pl.BlockSpec((1, units, width), at_expert),
                pl.BlockSpec((1, units, width), at_expert),
                pl.BlockSpec((1, tok, width), at_end),
            ],
            out_specs=pl.BlockSpec((1, rows, width), at_end),
            scratch_shapes=[
                pltpu.VMEM((experts, groups * spread, width), bf16),
                pltpu.VMEM((groups, cells, width), bf16),
                pltpu.VMEM((groups, rows, cells), bf16),
                pltpu.VMEM((groups, rows, known), f32),
            ],
        ),
        compiler_params=pltpu.CompilerParams(vmem_limit_bytes=56 << 20),
        name="experts",
    )(where, x, ids, router, cell_expert, cell_number, before, source, w_gate, w_up, w_down, shared)


def per_device(
    attn_heads,
    residual,
    w_out,
    gain_post,
    w_router,
    expert_ids,
    expert_slot,
    w_gate,
    w_up,
    w_down,
    w_shared_gate,
    w_shared_up,
    w_shared_down,
    w_shared_score,
    gain_final,
):
    groups = lax.axis_size("ep")
    z_count = groups // 2
    experts_here = w_gate.shape[0]
    expert_count = w_router.shape[1]
    width = residual.shape[2]
    tok = residual.shape[1]
    rows = N_DP * tok
    spread = N_DP * MOST
    known = -(-(expert_count + 1) // 64) * 64

    ids = jnp.swapaxes(expert_ids[0], 0, 1)
    ids = jnp.pad(ids, ((0, 8 - ids.shape[0]), (0, 128 - tok)))
    router = jnp.concatenate([w_router.T, w_shared_score[None, :]], axis=0)
    router = jnp.pad(router, ((0, known - expert_count - 1), (0, 0)))
    here = lax.axis_index("ep") * experts_here + jnp.arange(experts_here * spread, dtype=jnp.int32) // spread
    slots = jnp.pad(expert_slot, (0, known - expert_count), constant_values=-1)
    cell_expert = (here[:, None] == slots[None, :]).astype(bf16)

    x_all, hidden_state, ids_all, shared = project_and_gather(
        z_count, attn_heads[0], w_out, residual[0], gain_post.reshape(1, width), ids,
        w_shared_gate.T, w_shared_up.T, w_shared_down,
    )
    partial_sums = run_experts(
        x_all.reshape(groups, rows, width), ids_all, router, cell_expert, expert_count,
        jnp.swapaxes(w_gate, 1, 2), jnp.swapaxes(w_up, 1, 2), w_down, shared,
    )
    mixed_out, final_out = reduce_and_norm(
        z_count, partial_sums.reshape(groups * N_DP, tok, width), hidden_state,
        gain_final.reshape(1, width),
    )
    return (mixed_out[None], final_out[None])


def solution(mesh):
    in_specs = (
        P("ep", None, "dp"),
        P("ep", "dp", None),
        P("dp", None),
        P(),
        P(),
        P("ep", "dp", None),
        P(),
        P("ep", None, "dp"),
        P("ep", None, "dp"),
        P("ep", "dp", None),
        P(None, "ep"),
        P(None, "ep"),
        P("ep", None),
        P(),
        P(),
    )
    out_specs = (P("ep", "dp", None), P("ep", "dp", None))
    return jax.shard_map(
        per_device, mesh=mesh, in_specs=in_specs, out_specs=out_specs, check_vma=False
    )
```

```python
import functools

import jax
import jax.numpy as jnp
import numpy as np
from jax import lax
from jax.experimental import pallas as pl
from jax.experimental.pallas import tpu as pltpu
from jax.sharding import PartitionSpec as P

MOST = 8
N_DP = 4

eps_norm = 1e-06

f32 = jnp.float32
bf16 = jnp.bfloat16


def place(axes=("dp", "ep")):
    dp = lax.axis_index("dp")
    ep = lax.axis_index("ep")
    core = ep % 2
    z = ep // 2
    low = dp % 2
    high = dp // 2
    flip_low = 1 - 2 * low
    flip_high = 2 - 4 * high
    first = dp + (1 - core) * flip_low + core * flip_high
    second = dp + core * flip_low + (1 - core) * flip_high
    return dp, z, core, first, second, 3 - dp


def greet(z_count, dp, z, core):
    barrier = pltpu.get_barrier_semaphore()

    def hello(d, e):
        pl.semaphore_signal(barrier, inc=1, device_id={"dp": d, "ep": e})

    for k in range(1, N_DP):
        hello((dp + k) % N_DP, z * 2 + core)
    for k in range(1, z_count):
        hello(dp, ((z + k) % z_count) * 2 + core)
    hello(dp, z * 2 + 1 - core)
    pl.semaphore_wait(barrier, N_DP - 1 + z_count - 1 + 1)


def rows_dot(a, b):
    return lax.dot_general(a, b, (((1,), (1,)), ((), ())), preferred_element_type=f32)


def gather_kernel(
    z_count, tok, attn_hbm, w_out_hbm, residual, gain, ids, gate_hbm, up_hbm, down_hbm,
    rows, hidden, ids_out, shared,
    attn, w_out, outbox, inbox, own, names, gate_w, up_w, down_w, line,
    ps, pr, zs, zr, fs, fr, ss, sr, cs, cr, local, weight_sem, line_sem,
    izs, izr, ifs, ifr, iss, isr, ics, icr,
):
    dp, z, core, first, second, far = place()
    early = [
        pltpu.make_async_copy(src, dst, weight_sem.at[3 + i])
        for i, (src, dst) in enumerate(((w_out_hbm, w_out), (attn_hbm, attn)))
    ]
    for load in early:
        load.start()
    greet(z_count, dp, z, core)

    def send(src, dst, s_sem, r_sem, d, e):
        return pltpu.make_async_remote_copy(
            src_ref=src, dst_ref=dst, send_sem=s_sem, recv_sem=r_sem,
            device_id={"dp": d, "ep": e},
        )

    me = z * 2 + core
    pending = []
    projections = []
    loads = [
        pltpu.make_async_copy(src, dst, weight_sem.at[i])
        for i, (src, dst) in enumerate(((gate_hbm, gate_w), (up_hbm, up_w), (down_hbm, down_w)))
    ]
    for load in loads:
        load.start()

    def arrived(sem, ref):
        pltpu.make_async_copy(ref, ref, sem).wait()

    def go(copy):
        copy.start()
        pending.append(copy)

    names[core, dp, z] = ids[...]
    for k in range(1, z_count):
        spot = names.at[core, dp, z]
        go(send(spot, spot, izs.at[k], izr.at[k], dp, ((z + k) % z_count) * 2 + core))

    def names_step(step):
        if step == 0:
            for k in range(1, z_count):
                arrived(izr.at[k], names.at[core, dp, (z + z_count - k) % z_count])
            spot = names.at[core, dp]
            go(send(spot, spot, ifs.at[0], ifr.at[0], first, me))
        elif step == 1:
            arrived(ifr.at[0], names.at[core, first])
            for i, d in ((0, dp), (1, first)):
                spot = names.at[core, d]
                go(send(spot, spot, iss.at[i], isr.at[i], second, me))
        elif step == 2:
            arrived(isr.at[0], names.at[core, second])
            arrived(isr.at[1], names.at[core, far])
            spot = names.at[core]
            go(send(spot, spot, ics.at[0], icr.at[0], dp, z * 2 + 1 - core))

    for load in early:
        load.wait()
    for step, k in enumerate((2, 1, 3)):
        q = (dp + k) % N_DP
        outbox[k - 1] = jnp.dot(
            attn[pl.ds(pl.multiple_of(q * tok, tok), tok), :], w_out[...],
            preferred_element_type=f32,
        ).astype(bf16)
        copy = send(outbox.at[k - 1], inbox.at[k - 1], ps.at[k - 1], pr.at[k - 1], q, me)
        copy.start()
        projections.append((k, copy))
        names_step(step)
    total = residual[...].astype(f32) + jnp.dot(
        attn[pl.ds(pl.multiple_of(dp * tok, tok), tok), :], w_out[...],
        preferred_element_type=f32,
    )
    for k, copy in projections:
        copy.wait_recv()
        total = total + inbox[k - 1].astype(f32)
    state = total.astype(bf16)
    hidden[...] = state
    wide = state.astype(f32)
    own[...] = (
        wide * lax.rsqrt(jnp.mean(wide * wide, axis=-1, keepdims=True) + eps_norm)
        * gain[...].astype(f32)
    ).astype(bf16)
    for k, copy in projections:
        copy.wait_send()

    def block(k, c, d):
        return rows.at[(((z + z_count - k) % z_count) * 2 + c) * N_DP + d]

    keep = pltpu.make_async_copy(own, block(0, core, dp), local.at[0])
    keep.start()

    def over_first(k):
        src = own if k == 0 else block(k, core, dp)
        return send(src, block(k, core, dp), fs.at[k], fr.at[k], first, me)

    def over_second(k, j):
        d = dp if j == 0 else first
        src = own if k == 0 and j == 0 else block(k, core, d)
        return send(src, block(k, core, d), ss.at[2 * k + j], sr.at[2 * k + j], second, me)

    def over_core(k, j):
        d = (dp, first, second, far)[j]
        src = own if k == 0 and j == 0 else block(k, core, d)
        return send(src, block(k, core, d), cs.at[4 * k + j], cr.at[4 * k + j], dp, z * 2 + 1 - core)

    def share(c):
        for start in range(0, z_count, 4):
            some = range(start, min(start + 4, z_count))
            moves = []
            for i, k in enumerate(some):
                if c == 1:
                    arrived(cr.at[4 * k], block(k, 1 - core, dp))
                elif k == 0:
                    keep.wait()
                where = block(k, core if c == 0 else 1 - core, dp)
                move = pltpu.make_async_copy(where, line.at[pl.ds(i * tok, tok)], line_sem.at[i])
                move.start()
                moves.append(move)
            for move in moves:
                move.wait()
            count = len(moves) * tok
            x = line[:count]
            gate = rows_dot(x, gate_w[...])
            up = rows_dot(x, up_w[...])
            units = (gate / (1.0 + jnp.exp(-gate)) * up).astype(bf16)
            out = jnp.dot(units, down_w[...], preferred_element_type=f32).astype(bf16)
            for i, k in enumerate(some):
                level = (z + z_count - k) % z_count
                shared[level * 2 + (core if c == 0 else 1 - core)] = out[i * tok:(i + 1) * tok]

    go(over_first(0))
    go(over_second(0, 0))

    def along_z(k):
        if k < z_count:
            go(send(own, block(0, core, dp), zs.at[k], zr.at[k], dp, ((z + k) % z_count) * 2 + core))

    along_z(1)
    go(over_core(0, 0))

    def tail(k):
        for j, d in ((0, second), (1, far)):
            arrived(sr.at[2 * k + j], block(k, core, d))
            go(over_core(k, 2 + j))

    for k in range(z_count):
        if k > 0:
            arrived(zr.at[k], block(k, core, dp))
            along_z(k + 1)
            go(over_first(k))
            go(over_second(k, 0))
            go(over_core(k, 0))
        arrived(fr.at[k], block(k, core, first))
        go(over_second(k, 1))
        go(over_core(k, 1))
        if k == z_count - 1:
            for load in loads:
                load.wait()
            share(0)
        if k > 0:
            tail(k - 1)
    share(1)
    tail(z_count - 1)
    arrived(icr.at[0], names.at[1 - core])
    for c in range(2):
        for d in range(N_DP):
            for level in range(z_count):
                ids_out[level * 2 + c, :, d * tok:(d + 1) * tok] = names[c, d, level][:, :tok]
    for k in range(z_count):
        for j, d in ((1, second), (2, first), (3, far)):
            arrived(cr.at[4 * k + j], block(k, 1 - core, d))
    for copy in pending:
        copy.wait_send()


def project_and_gather(z_count, attn, w_out, residual, gain, ids, gate, up, down):
    units = down.shape[0]
    tok, width = residual.shape
    count = z_count * 2 * N_DP
    dma = pltpu.SemaphoreType.DMA
    vmem = pl.BlockSpec(memory_space=pltpu.VMEM)
    return pl.pallas_call(
        functools.partial(gather_kernel, z_count, tok),
        out_shape=(
            jax.ShapeDtypeStruct((count, tok, width), bf16),
            jax.ShapeDtypeStruct((tok, width), bf16),
            jax.ShapeDtypeStruct((z_count * 2, 8, N_DP * tok), jnp.int32),
            jax.ShapeDtypeStruct((z_count * 2, tok, width), bf16),
        ),
        in_specs=[pl.BlockSpec(memory_space=pl.ANY)] * 2 + [vmem] * 3
        + [pl.BlockSpec(memory_space=pl.ANY)] * 3,
        out_specs=(pl.BlockSpec(memory_space=pl.ANY), vmem, vmem, vmem),
        scratch_shapes=[
            pltpu.VMEM(attn.shape, bf16),
            pltpu.VMEM(w_out.shape, bf16),
            pltpu.VMEM((N_DP - 1, tok, width), bf16),
            pltpu.VMEM((N_DP - 1, tok, width), bf16),
            pltpu.VMEM((tok, width), bf16),
            pltpu.VMEM((2, N_DP, z_count, 8, 128), jnp.int32),
            pltpu.VMEM((units, width), bf16),
            pltpu.VMEM((units, width), bf16),
            pltpu.VMEM((units, width), bf16),
            pltpu.VMEM((4 * tok, width), bf16),
            dma((N_DP - 1,)), dma((N_DP - 1,)),
            dma((z_count,)), dma((z_count,)),
            dma((z_count,)), dma((z_count,)),
            dma((2 * z_count,)), dma((2 * z_count,)),
            dma((4 * z_count,)), dma((4 * z_count,)),
            dma((1,)), dma((5,)), dma((4,)),
            dma((z_count,)), dma((z_count,)),
            dma((1,)), dma((1,)),
            dma((2,)), dma((2,)),
            dma((1,)), dma((1,)),
        ],
        compiler_params=pltpu.CompilerParams(
            collective_id=0, has_side_effects=True, vmem_limit_bytes=48 << 20
        ),
        name="project_gather",
    )(attn, w_out, residual, gain, ids, gate, up, down)


def scatter_kernel(
    z_count, tok, results, back, shared, hidden, gain, mixed, final,
    res_buf, back_buf, shared_buf, whole, outbox, acc, from_core, from_second, from_first, from_z,
    loads, cs, cr, ss, sr, fs, fr, zs, zr,
):
    dp, z, core, first, second, far = place()
    me = z * 2 + core
    other = z * 2 + 1 - core
    pending = []
    order = sorted(range(1, z_count), key=lambda k: abs(2 * k - z_count)) + [0]

    def level(k):
        return (z + z_count - k) % z_count

    def arrived(sem, ref):
        pltpu.make_async_copy(ref, ref, sem).wait()

    def fetches(i):
        found = []
        for side in range(2):
            g = level(order[i]) * 2 + ((1 - core) if side == 0 else core)
            slot = 2 * (i % 2) + side
            for n, (src, dst) in enumerate(((results, res_buf), (back, back_buf), (shared, shared_buf))):
                found.append(pltpu.make_async_copy(src.at[g], dst.at[slot], loads.at[3 * slot + n]))
        return found

    for fetch in fetches(0):
        fetch.start()
    greet(z_count, dp, z, core)

    def send(src, dst, s_sem, r_sem, d, e):
        copy = pltpu.make_async_remote_copy(
            src_ref=src, dst_ref=dst, send_sem=s_sem, recv_sem=r_sem,
            device_id={"dp": d, "ep": e},
        )
        copy.start()
        return copy

    across = {}

    def combine(i, side):
        k = order[i]
        slot = 2 * (i % 2) + side
        dests = (dp, second, first, far) if side == 0 else (dp, first, second, far)
        for fetch in fetches(i)[3 * side:3 * side + 3]:
            fetch.wait()
        whole[...] = jnp.dot(back_buf[slot], res_buf[slot], preferred_element_type=f32).astype(bf16)
        for j in (3, 2, 1, 0):
            value = whole[pl.ds(pl.multiple_of(dests[j] * tok, tok), tok), :]
            if j == 0:
                value = (value.astype(f32) + shared_buf[slot].astype(f32)).astype(bf16)
            if side == 1:
                acc[4 * k + j] = value
            else:
                n = 4 * (i % 2) + j
                if i >= 2:
                    across[(i - 2, j)].wait_send()
                outbox[n] = value
                across[(i, j)] = send(
                    outbox.at[n], from_core.at[4 * k + j], cs.at[4 * k + j], cr.at[4 * k + j], dp, other
                )

    def prepare(i):
        if i + 1 < z_count:
            for fetch in fetches(i + 1):
                fetch.start()
        combine(i, 0)
        combine(i, 1)

    def pair(k, j):
        n = 4 * k + j
        arrived(cr.at[n], from_core.at[n])
        return acc[n].astype(f32) + from_core[n].astype(f32)

    def pass_second(k):
        for j in (3, 2):
            acc[4 * k + j] = pair(k, j).astype(bf16)
            n = 2 * k + j - 2
            pending.append(send(acc.at[4 * k + j], from_second.at[n], ss.at[n], sr.at[n], second, me))

    def summed(k, j):
        n = 2 * k + j
        value = pair(k, j)
        arrived(sr.at[n], from_second.at[n])
        return value + from_second[n].astype(f32)

    def pass_first(k):
        acc[4 * k + 1] = summed(k, 1).astype(bf16)
        pending.append(send(acc.at[4 * k + 1], from_first.at[k], fs.at[k], fr.at[k], first, me))

    def pass_z(k):
        value = summed(k, 0)
        arrived(fr.at[k], from_first.at[k])
        value = value + from_first[k].astype(f32)
        if k > 0:
            acc[4 * k] = value.astype(bf16)
            pending.append(
                send(acc.at[4 * k], from_z.at[k], zs.at[k], zr.at[k], dp, level(k) * 2 + core)
            )
        return value

    prepare(0)
    for i, k in enumerate(order):
        pass_second(k)
        if i + 1 < z_count:
            prepare(i + 1)
        if i > 0:
            pass_z(order[i - 1])
        pass_first(k)
    value = pass_z(0)
    for k in order[:-1]:
        arrived(zr.at[k], from_z.at[k])
        value = value + from_z[k].astype(f32)
    out = (hidden[...].astype(f32) + value).astype(bf16)
    mixed[...] = out
    wide = out.astype(f32)
    final[...] = (
        wide * lax.rsqrt(jnp.mean(wide * wide, axis=-1, keepdims=True) + eps_norm)
        * gain[...].astype(f32)
    ).astype(bf16)
    for copy in pending:
        copy.wait_send()
    for i in range(max(0, z_count - 2), z_count):
        for j in range(4):
            across[(i, j)].wait_send()


def reduce_and_norm(z_count, results, back, shared, hidden, gain):
    tok, width = hidden.shape
    _, rows, cells = back.shape
    dma = pltpu.SemaphoreType.DMA
    vmem = pl.BlockSpec(memory_space=pltpu.VMEM)
    shape = jax.ShapeDtypeStruct((tok, width), bf16)
    boxes = [8, 4 * z_count, 4 * z_count, 2 * z_count, z_count, z_count]
    sems = [12] + [4 * z_count] * 2 + [2 * z_count] * 2 + [z_count] * 4
    return pl.pallas_call(
        functools.partial(scatter_kernel, z_count, tok),
        out_shape=(shape, shape),
        in_specs=[pl.BlockSpec(memory_space=pl.ANY)] * 3 + [vmem, vmem],
        out_specs=(vmem, vmem),
        scratch_shapes=[
            pltpu.VMEM((4, cells, width), bf16),
            pltpu.VMEM((4, rows, cells), bf16),
            pltpu.VMEM((4, tok, width), bf16),
            pltpu.VMEM((rows, width), bf16),
        ]
        + [pltpu.VMEM((n, tok, width), bf16) for n in boxes]
        + [dma((n,)) for n in sems],
        compiler_params=pltpu.CompilerParams(
            collective_id=1, has_side_effects=True, vmem_limit_bytes=60 << 20
        ),
        name="reduce_norm",
    )(results, back, shared, hidden, gain)


def expert_kernel(
    groups, experts, tok, where_ref, x_ref, ids_ref, router_ref, cell_expert_ref, cell_number_ref,
    before_ref, source_ref, gate_ref, up_ref, down_ref, shared_ref,
    results_ref, back_ref, scaled_ref, cells, logits_ref,
):
    step = pl.program_id(0)
    wide = N_DP * MOST

    @pl.when(step < groups)
    def _():
        x = x_ref[0]
        logits = rows_dot(x, router_ref[...])
        logits_ref[...] = logits
        lined = logits.T
        numbers = lax.broadcasted_iota(jnp.int32, lined.shape, 0)
        chosen = numbers == ids_ref[0, 0:1, :]
        for k in range(1, 4):
            chosen = chosen | (numbers == ids_ref[0, k:k + 1, :])
        powers = jnp.where(chosen, jnp.exp(lined), 0.0)
        weights = (powers / jnp.sum(powers, axis=0, keepdims=True)).astype(bf16)
        hit = jnp.where(chosen, 1.0, 0.0).astype(bf16)
        rank = jnp.dot(hit, before_ref[...], preferred_element_type=f32) + source_ref[...]
        at_cell = cell_expert_ref[...]
        named = jnp.dot(at_cell, hit, preferred_element_type=f32)
        spot = jnp.dot(at_cell, rank.astype(bf16), preferred_element_type=f32)
        weight = jnp.dot(at_cell, weights, preferred_element_type=f32)
        here = (named > 0.5) & (spot == cell_number_ref[...])
        back_ref[0] = jnp.where(here, weight, 0.0).T.astype(bf16)
        picked = jnp.dot(
            jnp.where(here, 1.0, 0.0).astype(bf16), x, preferred_element_type=f32
        ).astype(bf16)
        for e in range(experts):
            cells[e, pl.ds(pl.multiple_of(step * wide, wide), wide), :] = picked[e * wide:(e + 1) * wide]
        columns = logits_ref[pl.ds(pl.multiple_of(where_ref[0] * tok, tok), tok), :]
        lane = lax.broadcasted_iota(jnp.int32, columns.shape, 1)
        score = jnp.sum(jnp.where(lane == where_ref[1], columns, 0.0), axis=1, keepdims=True)
        scaled_ref[0] = (shared_ref[0].astype(f32) / (1.0 + jnp.exp(-score))).astype(bf16)

    @pl.when(step >= groups)
    def _():
        e = step - groups
        rows = cells[e]
        gate = rows_dot(rows, gate_ref[0])
        up = rows_dot(rows, up_ref[0])
        hidden = (gate / (1.0 + jnp.exp(-gate)) * up).astype(bf16)
        result = jnp.dot(hidden, down_ref[0], preferred_element_type=f32).astype(bf16)
        for g in range(groups):
            results_ref[g] = result[g * wide:(g + 1) * wide]


def run_experts(x, ids, router, cell_expert, score_row, w_gate, w_up, w_down, shared):
    groups, rows, width = x.shape
    experts, units, _ = w_gate.shape
    cells, known = cell_expert.shape
    tok = rows // N_DP
    spread = N_DP * MOST
    place_of = np.arange(rows)
    before = (place_of[:, None] < place_of[None, :]) & (
        place_of[:, None] // tok == place_of[None, :] // tok
    )
    before = jnp.asarray(before, bf16)
    source = jnp.asarray(place_of[None, :] // tok * MOST, f32)
    cell_number = jnp.asarray(np.arange(cells)[:, None] % spread, f32)

    def at_group(i, *_):
        return (jnp.minimum(i, groups - 1), 0, 0)

    def at_expert(i, *_):
        return (jnp.clip(i - groups, 0, experts - 1), 0, 0)

    def at_slice(i, *_):
        return (0, jnp.clip(i - groups, 0, experts - 1), 0)

    def whole(i, *_):
        return (0, 0)

    where = jnp.stack([lax.axis_index("dp").astype(jnp.int32), jnp.int32(score_row)])
    return pl.pallas_call(
        functools.partial(expert_kernel, groups, experts, tok),
        out_shape=(
            jax.ShapeDtypeStruct((groups, cells, width), bf16),
            jax.ShapeDtypeStruct((groups, rows, cells), bf16),
            jax.ShapeDtypeStruct((groups, tok, width), bf16),
        ),
        grid_spec=pltpu.PrefetchScalarGridSpec(
            num_scalar_prefetch=1,
            grid=(groups + experts,),
            in_specs=[
                pl.BlockSpec((1, rows, width), at_group),
                pl.BlockSpec((1, 8, rows), at_group),
                pl.BlockSpec(router.shape, whole),
                pl.BlockSpec((cells, known), whole),
                pl.BlockSpec((cells, 1), whole),
                pl.BlockSpec((rows, rows), whole),
                pl.BlockSpec((1, rows), whole),
                pl.BlockSpec((1, units, width), at_expert),
                pl.BlockSpec((1, units, width), at_expert),
                pl.BlockSpec((1, units, width), at_expert),
                pl.BlockSpec((1, tok, width), at_group),
            ],
            out_specs=(
                pl.BlockSpec((groups, spread, width), at_slice),
                pl.BlockSpec((1, rows, cells), at_group),
                pl.BlockSpec((1, tok, width), at_group),
            ),
            scratch_shapes=[
                pltpu.VMEM((experts, groups * spread, width), bf16),
                pltpu.VMEM((rows, known), f32),
            ],
        ),
        compiler_params=pltpu.CompilerParams(vmem_limit_bytes=56 << 20),
        name="experts",
    )(where, x, ids, router, cell_expert, cell_number, before, source, w_gate, w_up, w_down, shared)


def per_device(
    attn_heads,
    residual,
    w_out,
    gain_post,
    w_router,
    expert_ids,
    expert_slot,
    w_gate,
    w_up,
    w_down,
    w_shared_gate,
    w_shared_up,
    w_shared_down,
    w_shared_score,
    gain_final,
):
    groups = lax.axis_size("ep")
    z_count = groups // 2
    experts_here = w_gate.shape[0]
    expert_count = w_router.shape[1]
    width = residual.shape[2]
    tok = residual.shape[1]
    rows = N_DP * tok
    spread = N_DP * MOST
    known = -(-(expert_count + 1) // 64) * 64

    ids = jnp.swapaxes(expert_ids[0], 0, 1)
    ids = jnp.pad(ids, ((0, 8 - ids.shape[0]), (0, 128 - tok)))
    router = jnp.concatenate([w_router.T, w_shared_score[None, :]], axis=0)
    router = jnp.pad(router, ((0, known - expert_count - 1), (0, 0)))
    here = lax.axis_index("ep") * experts_here + jnp.arange(experts_here * spread, dtype=jnp.int32) // spread
    slots = jnp.pad(expert_slot, (0, known - expert_count), constant_values=-1)
    cell_expert = (here[:, None] == slots[None, :]).astype(bf16)

    x_all, hidden_state, ids_all, shared = project_and_gather(
        z_count, attn_heads[0], w_out, residual[0], gain_post.reshape(1, width), ids,
        w_shared_gate.T, w_shared_up.T, w_shared_down,
    )
    results, back, scaled = run_experts(
        x_all.reshape(groups, rows, width), ids_all, router, cell_expert, expert_count,
        jnp.swapaxes(w_gate, 1, 2), jnp.swapaxes(w_up, 1, 2), w_down, shared,
    )
    mixed_out, final_out = reduce_and_norm(
        z_count, results, back, scaled, hidden_state, gain_final.reshape(1, width),
    )
    return (mixed_out[None], final_out[None])


def solution(mesh):
    in_specs = (
        P("ep", None, "dp"),
        P("ep", "dp", None),
        P("dp", None),
        P(),
        P(),
        P("ep", "dp", None),
        P(),
        P("ep", None, "dp"),
        P("ep", None, "dp"),
        P("ep", "dp", None),
        P(None, "ep"),
        P(None, "ep"),
        P("ep", None),
        P(),
        P(),
    )
    out_specs = (P("ep", "dp", None), P("ep", "dp", None))
    return jax.shard_map(
        per_device, mesh=mesh, in_specs=in_specs, out_specs=out_specs, check_vma=False
    )
```
